128 devices in a mesh: pop: 4 (over y), hap: 8 (over z_hi, x), blk: 4 (over z_lo, core).
Axes of the slice: x: 4, y: 4, z: 4 (z_hi: 2, z_lo: 2; z = z_hi * 2 + z_lo), core: 2. Of those that a mesh axis runs over, the one named last changes fastest.
Arguments:
- panels: bfloat16 [4, 16384, 16384], P('pop', ('hap', 'blk')), may hold values from 0 to 1
- counts: int32 [4], P('pop'), may hold values from 4096 to 16384, as said below
- marginal: float32 [4, 64, 16384], P('pop', None, ('hap', 'blk')), may hold values from -6 to 6
- shrink: float32 [16384], P(('hap', 'blk')), may hold values from 0.2 to 2
Outputs:
- posterior: float32 [4, 64, 16384], P('pop', None, ('hap', 'blk'))
- combined: float32 [64, 16384], P(None, ('hap', 'blk'))
The draws below stay inside these ranges and needn't reach their ends.
Inputs may be any that keep to these rules, and one draw needn't show every extreme that they name: `counts`: one population has all 16384 rows.
All inputs are finite; a program needn't handle non-finite values.
Results may differ from the reference program's by a relative error of at most 0.0003.
Values may be sent and summed in bfloat16 or wider, within the bound.
No kernel may reach another device: no remote copies, remote signals or barrier semaphores. Data moves between devices by JAX's collectives and lax.ppermute only.
A program may use at most 192 MiB of HBM per device.

```python
import math
import jax
import jax.numpy as jnp
from jax import lax

BLOCK = 512
TRAITS = 64
HAP_DEV = 512
POPS = 4
SNPS = 16384
HAPS = 16384


def draw_panels(key, part):
    per_pop = HAPS // HAP_DEV

    def one(group):
        pop_index = group // per_pop
        pop_key = jax.random.fold_in(key, pop_index)
        key_found, key_thr = jax.random.split(pop_key)
        key_offset = jax.random.fold_in(pop_key, 5)
        offset = jax.random.randint(key_offset, (), 0, 64)
        rare_cols = (jnp.arange(SNPS) + offset) % 64 == 0
        thresh = jax.random.randint(key_thr, (SNPS,), 3, 500)
        founders = (jax.random.randint(key_found, (32, SNPS), 0, 1000) < thresh[None, :]).astype(jnp.int32)
        group_key = jax.random.fold_in(key, 100000 + group)
        key_anc, key_flip, key_noise = jax.random.split(group_key, 3)
        key_small = jax.random.fold_in(group_key, 9)
        row_ids = group % per_pop * HAP_DEV + jnp.arange(HAP_DEV)
        lowest = row_ids * 24 // HAPS
        ancestry = lowest[:, None] + jax.random.randint(key_anc, (HAP_DEV, SNPS // 16), 0, 8)
        ancestry = jnp.repeat(ancestry, 16, axis=1)
        alleles = jnp.take_along_axis(founders, ancestry, axis=0)
        flips = (jax.random.randint(key_flip, (HAP_DEV, SNPS), 0, 50) == 0).astype(jnp.int32)
        alleles = jnp.bitwise_xor(alleles, flips)
        noise = jax.random.uniform(key_noise, (HAP_DEV, SNPS), jnp.float32, 0.0, 0.15)
        small_noise = jax.random.uniform(key_small, (HAP_DEV, SNPS), jnp.float32, 0.0, 0.05)
        value = jnp.where(alleles == 1, 1.0 - noise, noise)
        value = jnp.where(rare_cols[None, :], small_noise, value)
        return value.astype(jnp.bfloat16)
    result = lax.map(one, jnp.arange(POPS * per_pop))
    return result.reshape(POPS, HAPS, SNPS)


def draw_counts(key, part):
    key_vals, key_top = jax.random.split(jax.random.fold_in(key, 7))
    values = jax.random.randint(key_vals, (POPS,), HAPS // 4, HAPS + 1)
    chosen = jax.random.randint(key_top, (), 0, POPS)
    return jnp.where(jnp.arange(POPS) == chosen, HAPS, values).astype(jnp.int32)


def level_of(own_key, shape, pieces, smallest, top_value):
    def one(axis_at, blocks):
        steps = jax.random.uniform(jax.random.fold_in(jax.random.fold_in(own_key, 6), axis_at), (blocks,), jnp.float32, smallest / len(pieces), top_value / len(pieces))
        return jnp.repeat(jnp.exp(steps), shape[axis_at] // blocks).reshape((-1,) + (1,) * (len(shape) - axis_at - 1))

    factor_of = one(*pieces[0])
    for cut in pieces[1:]:
        factor_of = factor_of * one(*cut)
    return factor_of


def normal_values(rng, dims, width, limit, pieces=(), kind=jnp.bfloat16):
    loudness = level_of(rng, dims, pieces, -0.22, 0.18) if pieces else 1.0
    values = jax.random.normal(rng, dims, jnp.float32) * width * loudness
    return jnp.minimum(jnp.maximum(values, -limit), limit).astype(kind)


def setup_inputs(seed: int = 0) -> dict:
    seeds = jax.random.split(jax.random.key(seed), 5)
    panels = draw_panels(jax.random.fold_in(seeds[4], 71), 0)
    counts = draw_counts(jax.random.fold_in(seeds[4], 71), 0)
    marginal = normal_values(seeds[2], (POPS, TRAITS, SNPS), 1.0, 6.0, ((0, 4), (2, 32)), jnp.float32)
    shrink = jnp.clip(jnp.exp(math.log(2.0) - 2.3025851 * jax.random.uniform(seeds[3], (SNPS,), jnp.float32) ** level_of(seeds[3], (SNPS,), ((0, 32),), -0.2, 0.2)), 0.2, 2.0)
    return {"panels": panels, "counts": counts, "marginal": marginal, "shrink": shrink}


def block_solve(gram, colsum, count, shrink_part, rhs):
    freq = colsum / count
    cov = gram / count - freq[:, None] * freq[None, :]
    spread = jnp.sqrt(jnp.maximum(jnp.diagonal(cov), 0.01))
    system = cov / (spread[:, None] * spread[None, :]) + jnp.diag(shrink_part)
    factor = jnp.linalg.cholesky(system)
    middle = lax.linalg.triangular_solve(factor, rhs.T, left_side=True, lower=True)
    answer = lax.linalg.triangular_solve(factor, middle, left_side=True, lower=True, transpose_a=True)
    return answer.T

def reference(panels, counts, marginal, shrink):
    nblk = SNPS // BLOCK

    def one(item):
        pop_index = (item // nblk).astype(jnp.int32)
        blk_index = (item % nblk).astype(jnp.int32)
        start = (blk_index * BLOCK).astype(jnp.int32)
        zero = jnp.zeros((), jnp.int32)
        cols = lax.dynamic_slice(panels, (pop_index, zero, start), (1, HAPS, BLOCK))[0]
        count_int = counts[pop_index]
        keep = (jnp.arange(HAPS).astype(jnp.int32) < count_int)[:, None]
        masked = jnp.where(keep, cols, jnp.zeros_like(cols))
        colsum = lax.optimization_barrier(jnp.sum(masked, axis=0, dtype=jnp.float32))
        gram = lax.dot_general(masked.astype(jnp.float32), masked.astype(jnp.float32), (((0,), (0,)), ((), ())), preferred_element_type=jnp.float32)
        rhs = lax.dynamic_slice(marginal, (pop_index, zero, start), (1, TRAITS, BLOCK))[0]
        shrink_part = lax.dynamic_slice(shrink, (start,), (BLOCK,))
        return block_solve(gram, colsum, count_int.astype(jnp.float32), shrink_part, rhs)
    items = jnp.arange(POPS * nblk).astype(jnp.int32)
    results = lax.map(one, items)
    results = results.reshape(POPS, nblk, TRAITS, BLOCK)
    posterior = jnp.transpose(results, (0, 2, 1, 3)).reshape(POPS, TRAITS, SNPS)
    weights = counts.astype(jnp.float32)
    combined = lax.optimization_barrier(jnp.sum(posterior * weights[:, None, None], axis=0)) / jnp.sum(weights)
    return (posterior, combined)
```

```python
import functools

import jax
import jax.numpy as jnp
from jax import lax
from jax.experimental import pallas as pl
from jax.experimental.pallas import tpu as pltpu
from jax.sharding import PartitionSpec as P


WIDTH = 512
HALF = 256
ROWS = 520
CUT = 264
RING = 4
AXES = ("hap", "blk")
ORDER = (
    (2, 2), (2, 1), (2, 3), (2, 0),
    (3, 3), (1, 2), (1, 1),
    (3, 2), (3, 1), (1, 3), (3, 0), (1, 0), (0, 2), (0, 1), (0, 3), (0, 0),
)
MAX_STEPS = 9
F32 = jnp.float32
BF16 = jnp.bfloat16


def chip_of(rank):
    hap, blk = rank // 4, rank % 4
    return hap % 4, (hap // 4) * 2 + blk // 2, blk % 2


def rank_of(x, z, core):
    return ((z // 2) * 4 + x) * 4 + (z % 2) * 2 + core


def ring_pairs(stage, step):
    pairs = []
    for rank in range(32):
        x, z, core = chip_of(rank)
        if (core == 0) == (stage == 0):
            x = (x + step) % RING
        else:
            z = (z + step) % RING
        pairs.append((rank, rank_of(x, z, core)))
    return pairs


def shift(value, stage, step):
    return lax.ppermute(value, AXES, ring_pairs(stage, step))


def swap_cores(value):
    return lax.ppermute(value, AXES, [(rank, rank ^ 1) for rank in range(32)])


def pack_kernel(table_ref, in_ref, out_ref):
    out_ref[0] = in_ref[...]


def pack(table, dosage, start, stop):
    rows = dosage.shape[0]
    return pl.pallas_call(
        pack_kernel,
        grid_spec=pltpu.PrefetchScalarGridSpec(
            num_scalar_prefetch=1,
            grid=(stop - start,),
            in_specs=[pl.BlockSpec((rows, WIDTH), lambda i, t: (0, t[16 + start + i]))],
            out_specs=pl.BlockSpec((1, rows, WIDTH), lambda i, t: (i, 0, 0)),
        ),
        out_shape=jax.ShapeDtypeStruct((stop - start, rows, WIDTH), dosage.dtype),
        cost_estimate=pl.CostEstimate(
            flops=0, bytes_accessed=(stop - start) * rows * WIDTH * 4, transcendentals=0
        ),
        name="pack",
    )(table, dosage)


def transposed_dot(left, right):
    return lax.dot_general(left, right, (((0,), (0,)), ((), ())), preferred_element_type=F32)


def gram_kernel(bounds, table_ref, own_ref, other_ref, *refs):
    out_refs, stacked = refs[:-1], refs[-1]
    rows = own_ref.shape[0]
    step = pl.program_id(0)
    ids = lax.broadcasted_iota(jnp.int32, (rows, WIDTH), 0)
    zero = jnp.zeros((), BF16)
    stacked[:rows, :] = jnp.where(ids < table_ref[32], own_ref[...], zero)
    stacked[rows:, :] = jnp.where(ids < table_ref[33], other_ref[0], zero)
    left, right = stacked[:, :HALF], stacked[:, HALF:]
    cross = transposed_dot(left, right)
    first = transposed_dot(left, left)
    second = transposed_dot(right, right)
    ones = jnp.ones((8, 2 * rows), BF16)
    sums = jnp.dot(ones, stacked[...], preferred_element_type=F32)
    row = lax.broadcasted_iota(jnp.int32, (HALF, HALF), 0)
    col = lax.broadcasted_iota(jnp.int32, (HALF, HALF), 1)
    folded = jnp.where(row > col, first, second)
    diagonal = jnp.sum(jnp.where(row == col, first, 0.0), axis=0, keepdims=True)
    pick = lax.broadcasted_iota(jnp.int32, (8, HALF), 0)
    tail = jnp.where(
        pick == 0,
        jnp.broadcast_to(diagonal, (8, HALF)),
        jnp.where(pick == 1, sums[:, :HALF], jnp.where(pick == 2, sums[:, HALF:], 0.0)),
    )
    for (low, high), out_ref in zip(bounds, out_refs):
        @pl.when((step >= low) & (step < high))
        def _(out_ref=out_ref):
            out_ref[0, :HALF, :] = cross
            out_ref[0, HALF : 2 * HALF, :] = folded
            out_ref[0, 2 * HALF :, :] = tail


def grams(table, dosage, other, start, base, sizes):
    rows = dosage.shape[0]
    bounds, low = [], 0
    for size in sizes:
        bounds.append((low, low + size))
        low += size
    total = low

    def out_map(low, size):
        return lambda i, t: (jnp.clip(i - low, 0, size - 1), 0, 0)

    return pl.pallas_call(
        functools.partial(gram_kernel, tuple(bounds)),
        grid_spec=pltpu.PrefetchScalarGridSpec(
            num_scalar_prefetch=1,
            grid=(total,),
            in_specs=[
                pl.BlockSpec((rows, WIDTH), lambda i, t: (0, t[start + i])),
                pl.BlockSpec((1, rows, WIDTH), lambda i, t: (start - base + i, 0, 0)),
            ],
            out_specs=[
                pl.BlockSpec((1, ROWS, HALF), out_map(low, high - low)) for low, high in bounds
            ],
            scratch_shapes=[pltpu.VMEM((2 * rows, WIDTH), BF16)],
        ),
        out_shape=[jax.ShapeDtypeStruct((size, ROWS, HALF), F32) for size in sizes],
        cost_estimate=pl.CostEstimate(
            flops=total * 4 * rows * WIDTH * WIDTH,
            bytes_accessed=total * (4 * rows * WIDTH + 4 * ROWS * HALF),
            transcendentals=0,
        ),
        name="gram",
    )(table, dosage, other)


def high_low(value):
    high = value.astype(BF16)
    return high, (value - high.astype(F32)).astype(BF16)


def mm(left, right):
    return jnp.dot(left, right, preferred_element_type=F32)


def solve_kernel(
    count_ref, own_ref, a_ref, b_ref, top0_ref, top1_ref, low0_ref, low1_ref,
    rhs_ref, shrink_ref, effects_ref, weighted_ref, full_ref, high_ref, low_ref,
):
    traits = rhs_ref.shape[0]
    count = count_ref[0].astype(F32)
    scale = jnp.full((1, WIDTH), 1.0, F32) / jnp.full((1, WIDTH), count, F32)
    top = own_ref[0, :CUT] + a_ref[0, :CUT] + b_ref[0, :CUT] + top0_ref[...] + top1_ref[...]
    bottom = own_ref[0, CUT:] + a_ref[0, CUT:] + b_ref[0, CUT:] + low0_ref[...] + low1_ref[...]
    full_ref[:CUT, :HALF] = top
    full_ref[CUT:ROWS, :HALF] = bottom
    cross = full_ref[:HALF, :HALF]
    folded = full_ref[HALF : 2 * HALF, :HALF]
    tail = full_ref[2 * HALF : ROWS, :HALF]
    row = lax.broadcasted_iota(jnp.int32, (HALF, HALF), 0)
    col = lax.broadcasted_iota(jnp.int32, (HALF, HALF), 1)
    eye = row == col
    diag0 = tail[0:1]
    diag1 = jnp.sum(jnp.where(eye, folded, 0.0), axis=0, keepdims=True)
    below = jnp.where(row > col, folded, 0.0)
    first = below + below.T + jnp.where(eye, jnp.broadcast_to(diag0, (HALF, HALF)), 0.0)
    above = jnp.where(row < col, folded, 0.0)
    second = above + above.T + jnp.where(eye, folded, 0.0)
    freq = jnp.concatenate([tail[1:2], tail[2:3]], axis=1) * scale
    variance = jnp.concatenate([diag0, diag1], axis=1) * scale - freq * freq
    variance = jnp.maximum(variance, 0.01)
    inverse = lax.rsqrt(variance)
    inverse = inverse * (1.5 - 0.5 * variance * inverse * inverse)
    pick = lax.broadcasted_iota(jnp.int32, (128, WIDTH), 0)
    columns = jnp.where(pick == 0, jnp.broadcast_to(freq, (128, WIDTH)), jnp.broadcast_to(inverse, (128, WIDTH))).T
    freq_col, inverse_col = columns[:, 0:1], columns[:, 1:2]
    full_ref[:HALF, :HALF] = first
    full_ref[:HALF, HALF:] = cross
    full_ref[HALF : 2 * HALF, :HALF] = cross.T
    full_ref[HALF : 2 * HALF, HALF:] = second
    wide_row = lax.broadcasted_iota(jnp.int32, (WIDTH, WIDTH), 0)
    wide_col = lax.broadcasted_iota(jnp.int32, (WIDTH, WIDTH), 1)
    shrink = shrink_ref[...]
    system = (full_ref[:WIDTH, :] * scale - freq_col * freq) * (inverse_col * inverse)
    system = system + jnp.where(wide_row == wide_col, jnp.broadcast_to(shrink, (WIDTH, WIDTH)), 0.0)
    bound = jnp.max(jnp.sum(jnp.abs(system), axis=0, keepdims=True), axis=1, keepdims=True)
    ratio = jnp.min(shrink, axis=1, keepdims=True) / bound
    factors, left = [], []
    for _ in range(MAX_STEPS):
        factors.append(2.0 / (1.0 + ratio))
        ratio = 4.0 * ratio / ((1.0 + ratio) * (1.0 + ratio))
        left.append(1.0 - ratio)
    scaled = system * (factors[0] / bound)
    full_ref[:WIDTH, :] = scaled
    high_ref[:WIDTH], low_ref[:WIDTH] = high_low(scaled)
    answer = rhs_ref[...] / bound
    full_ref[WIDTH:, :] = answer
    high_ref[WIDTH:], low_ref[WIDTH:] = high_low(answer)

    def step(k):
        value = full_ref[...]
        high, low = high_ref[...], low_ref[...]
        product = mm(high, high[:WIDTH]) + (mm(high, low[:WIDTH]) + mm(low, high[:WIDTH]))
        update = 2.0 * value - product
        answer = update[WIDTH:] * factors[k]
        full_ref[WIDTH:, :] = answer
        if k + 1 < MAX_STEPS:
            scaled = update[:WIDTH] * factors[k + 1]
            full_ref[:WIDTH, :] = scaled
            high_ref[:WIDTH], low_ref[:WIDTH] = high_low(scaled)
            high_ref[WIDTH:], low_ref[WIDTH:] = high_low(answer)

    for k in range(MAX_STEPS):
        if k < 6:
            step(k)
        else:
            @pl.when(jnp.max(left[k - 1]) > 1e-6)
            def _(k=k):
                step(k)

    answer = full_ref[WIDTH:, :]
    effects_ref[0] = answer
    weighted_ref[:traits, :] = answer * count
    weighted_ref[traits:, :] = jnp.full((8, WIDTH), count, F32)


def solve(count, own, a, b, tops, lows, rhs, shrink):
    traits = rhs.shape[0]
    block = pl.BlockSpec((1, ROWS, HALF), lambda i, n: (0, 0, 0))
    top = pl.BlockSpec((CUT, HALF), lambda i, n: (0, 0))
    low = pl.BlockSpec((ROWS - CUT, HALF), lambda i, n: (0, 0))
    return pl.pallas_call(
        solve_kernel,
        grid_spec=pltpu.PrefetchScalarGridSpec(
            num_scalar_prefetch=1,
            grid=(1,),
            in_specs=[
                pl.BlockSpec((1, ROWS, HALF), lambda i, n: (own.shape[0] - 1, 0, 0)),
                block, block, top, top, low, low,
                pl.BlockSpec((traits, WIDTH), lambda i, n: (0, 0)),
                pl.BlockSpec((1, WIDTH), lambda i, n: (0, 0)),
            ],
            out_specs=[
                pl.BlockSpec((1, traits, WIDTH), lambda i, n: (0, 0, 0)),
                pl.BlockSpec((traits + 8, WIDTH), lambda i, n: (0, 0)),
            ],
            scratch_shapes=[
                pltpu.VMEM((WIDTH + traits, WIDTH), F32),
                pltpu.VMEM((WIDTH + traits, WIDTH), BF16),
                pltpu.VMEM((WIDTH + traits, WIDTH), BF16),
            ],
        ),
        out_shape=[
            jax.ShapeDtypeStruct((1, traits, WIDTH), F32),
            jax.ShapeDtypeStruct((traits + 8, WIDTH), F32),
        ],
        cost_estimate=pl.CostEstimate(
            flops=7 * 6 * WIDTH**3, bytes_accessed=4 * 2**20, transcendentals=WIDTH
        ),
        name="solve",
    )(count, own, a, b, *tops, *lows, rhs, shrink)


def tables(rank, count, rows):
    x, z, core = chip_of(rank)
    first = jnp.array([d for d, _ in ORDER], jnp.int32)
    second = jnp.array([d for _, d in ORDER], jnp.int32)

    def owners(core):
        along_x = jnp.where(core == 0, first, second)
        along_z = jnp.where(core == 0, second, first)
        return rank_of((x + along_x) % RING, (z + along_z) % RING, core)

    ranks = jnp.array([rank, rank ^ 1])
    held = jnp.clip(count - ranks * rows, 0, rows)
    return jnp.concatenate([owners(core), owners(1 - core), held]).astype(jnp.int32)


def after(value, *others):
    return lax.optimization_barrier((value,) + others)[0]


def per_device(panels, counts, marginal, shrink):
    dosage = panels[0]
    rank = lax.axis_index(AXES)
    table = tables(rank, counts[0], dosage.shape[0])
    near = swap_cores(pack(table, dosage, 0, 4))
    far = swap_cores(pack(table, dosage, 4, 16))
    m1_minus, m1_plus = grams(table, dosage, near, 0, 0, (2, 2))
    r1_minus = shift(m1_minus, 0, -1)
    r1_plus = shift(m1_plus, 0, 1)
    m2_minus, m2_plus = grams(table, dosage, far, 4, 4, (1, 2))
    r2_minus = shift(m2_minus, 0, -1)
    r2_plus = shift(m2_plus, 0, 1)
    g3, g1, m4_minus, g10, own = grams(table, dosage, far, 7, 4, (2, 1, 1, 1, 4))
    m3_minus = g3 + r1_minus
    m3_plus = g1 + r1_plus[:1]
    r3_minus = shift(m3_minus, 0, -1)
    r3_plus = shift(m3_plus, 0, 1)
    r4_minus = shift(after(m4_minus, m3_minus), 0, -1)
    r4_plus = shift(g10 + r1_plus[1:], 0, 1)
    c2 = own[0] + r2_plus[0] + r3_minus[0]
    c1 = own[1] + r2_plus[1] + r3_minus[1]
    c3 = own[2] + r2_minus[0] + r3_plus[0]
    s3_minus = shift(c2[:CUT], 1, -1)
    s3_plus = shift(c2[CUT:], 1, 1)
    low0 = shift(c3[CUT:], 1, -1)
    top0 = shift(c1[:CUT], 1, 1)
    top1 = shift(c3[:CUT] + s3_minus, 1, -1)
    low1 = shift(c1[CUT:] + s3_plus, 1, 1)
    effects, weighted = solve(
        counts, own, r4_minus, r4_plus, (top0, top1), (low0, low1), marginal[0], shrink[None]
    )
    pops = lax.axis_size("pop")
    opposite, following, preceding = (
        lax.ppermute(weighted, "pop", [(i, (i + step) % pops) for i in range(pops)])
        for step in (2, 1, 3)
    )
    total = (weighted + opposite) + (following + preceding)
    traits = marginal.shape[1]
    return (effects, total[:traits] / total[traits : traits + 1])


def solution(mesh):
    placed = (
        P("pop", AXES, None),
        P("pop"),
        P("pop", None, AXES),
        P(AXES),
    )
    return jax.shard_map(
        per_device,
        mesh=mesh,
        in_specs=placed,
        out_specs=(P("pop", None, AXES), P(None, AXES)),
        check_vma=False,
    )
```
